32 devices in a mesh: section: 4 (over x, core), sp: 8 (over z, y).
Axes of the slice: x: 2, y: 2, z: 4, core: 2. Of those that a mesh axis runs over, the one named last changes fastest.
Arguments:
- field_in: bfloat16 [4, 384, 192, 768], P('section', 'sp'), may hold values from -6 to 6
- spectral_gain: bfloat16 [4, 192], P('section'), may hold values from 0.5 to 1.5
- spectral_weight: bfloat16 [4, 384, 192, 384], P('section', 'sp'), may hold values from -0.3125 to 0.3125
- mixer_gain: bfloat16 [4, 192], P('section'), may hold values from 0.5 to 1.5
- up_weight: bfloat16 [4, 192, 384], P('section'), may hold values from -0.4375 to 0.4375
- up_bias: bfloat16 [4, 384], P('section'), may hold values from -3 to 3
- down_weight: bfloat16 [4, 192, 384], P('section'), may hold values from -0.3125 to 0.3125
Outputs:
- next_field: bfloat16 [4, 384, 192, 768], P('section', 'sp')
The draws below stay inside these ranges and needn't reach their ends.
All inputs are finite; a program needn't handle non-finite values.
Results may differ from the reference program's by a relative error of at most 0.012.
Values may be sent and summed in bfloat16 or wider, within the bound.
A program may use at most 192 MiB of HBM per device.

```python
import math
import jax
import jax.numpy as jnp
from jax import lax

C = 192
HID = 384
NLAT = 384
NLON = 768
LMAX = 384
MMAX = 384
SECTIONS = 4


def shard_levels(rng, extent, split, smallest, top_value):
    def one(dim, shards_of):
        draws = jax.random.uniform(jax.random.fold_in(jax.random.fold_in(rng, 6), dim), (shards_of,), jnp.float32, smallest / len(split), top_value / len(split))
        return jnp.repeat(jnp.exp(draws), extent[dim] // shards_of).reshape((-1,) + (1,) * (len(extent) - dim - 1))

    level = one(*split[0])
    for cut in split[1:]:
        level = level * one(*cut)
    return level


def scatter_about(rng, dims, scale, most, pieces=(), kind=jnp.bfloat16):
    values = jax.random.normal(rng, dims, jnp.float32) * scale
    if len(pieces) > 0:
        values = shard_levels(rng, dims, pieces, -0.22, 0.18) * values
    return jnp.clip(values, min=-most, max=most).astype(kind)


def setup_inputs(seed: int = 0) -> dict:
    streams_of = jax.random.split(jax.random.key(seed), 8)
    return {
        "field_in": scatter_about(streams_of[0], (SECTIONS, NLAT, C, NLON), 1.0, 6.0, ((0, 4), (1, 8))),
        "spectral_gain": jnp.clip(1.0 + 0.1 * jax.random.normal(streams_of[1], (SECTIONS, C), jnp.float32), 0.5, 1.5).astype(jnp.bfloat16),
        "spectral_weight": scatter_about(streams_of[2], (SECTIONS, LMAX, C, 2 * C), (2 * C) ** -0.5, 0.3125, ((0, 4), (1, 8))),
        "mixer_gain": jnp.clip(1.0 + 0.1 * jax.random.normal(streams_of[3], (SECTIONS, C), jnp.float32), 0.5, 1.5).astype(jnp.bfloat16),
        "up_weight": scatter_about(streams_of[4], (SECTIONS, C, HID), C ** -0.5, 0.4375, ((0, 4),)),
        "up_bias": scatter_about(streams_of[5], (SECTIONS, HID), 0.5, 3.0, ((0, 4),)),
        "down_weight": scatter_about(streams_of[6], (SECTIONS, C, HID), HID ** -0.5, 0.3125, ((0, 4),)),
    }


EPSILON = 1e-05

def quad_weights(cycle_index, cycle_count):
    terms_count = cycle_count // 2
    orders = jnp.arange(1, terms_count + 1, dtype=jnp.int32)
    phase_turns = orders[None, :] * (2 * cycle_index[:, None] + 1) % (2 * cycle_count)
    angles = math.pi * phase_turns.astype(jnp.float32) / cycle_count
    orders_real = orders.astype(jnp.float32)
    series = lax.optimization_barrier(jnp.sum(jnp.cos(angles) / (4.0 * orders_real * orders_real - 1.0)[None, :], axis=1))
    return 2.0 / cycle_count * (1.0 - 2.0 * series)

def fourier_tables(point_count, orders):
    points = jnp.arange(point_count, dtype=jnp.int32)
    phase_turns = points[:, None] * orders[None, :] % point_count
    angles = 2.0 * math.pi / point_count * phase_turns.astype(jnp.float32)
    cosines = jnp.cos(angles)
    sine_values = jnp.sin(angles)
    forward = jnp.stack([cosines, -sine_values], axis=1).astype(jnp.bfloat16)
    doubling = jnp.where(orders == 0, 1.0, 2.0).astype(jnp.float32)[:, None]
    inverse = jnp.stack([cosines.T * doubling, -sine_values.T * doubling], axis=0).astype(jnp.bfloat16)
    return (forward, inverse)

def step_entries(degree, order_col, cosines):
    active = degree >= order_col + 1.0
    further = degree >= order_col + 2.0
    degree_sq = degree * degree
    order_sq = order_col * order_col
    lead_coeff = jnp.sqrt(jnp.where(active, (4.0 * degree_sq - 1.0) / jnp.where(active, degree_sq - order_sq, 1.0), 0.0))
    before = degree - 1.0
    before_sq = before * before
    trail_coeff = jnp.sqrt(jnp.where(further, (before_sq - order_sq) / jnp.where(further, 4.0 * before_sq - 1.0, 1.0), 0.0))
    diag_top = jnp.where(active, lead_coeff * cosines, 1.0)
    off_top = jnp.where(active, -lead_coeff * trail_coeff, 0.0)
    off_low = jnp.where(active, 1.0, 0.0)
    diag_low = jnp.where(active, 0.0, 1.0)
    return (diag_top, off_top, off_low, diag_low)

def legendre_rows(order_index, cycle_count, degree_count):
    colatitude = math.pi * (jnp.arange(cycle_count, dtype=jnp.float32) + 0.5) / cycle_count
    cosines = jnp.cos(colatitude)[None, None, :]
    sine_values = jnp.sin(colatitude)
    order_real = order_index.astype(jnp.float32)
    steps_all = jnp.arange(1, degree_count + 1, dtype=jnp.float32)
    factors = jnp.log((2.0 * steps_all - 1.0) / (2.0 * steps_all))
    below_mask = (steps_all[None, :] <= order_real[:, None]).astype(jnp.float32)
    partial_log = lax.optimization_barrier(jnp.sum(below_mask * factors[None, :], axis=1))
    start_log = 0.5 * jnp.log((2.0 * order_real + 1.0) / (4.0 * math.pi)) + 0.5 * partial_log
    start_log = start_log[:, None] + order_real[:, None] * jnp.log(sine_values)[None, :]
    order_col = order_real[None, :, None]
    block_count = degree_count // 16
    block_base = (16 * jnp.arange(block_count, dtype=jnp.int32)).astype(jnp.float32)[:, None, None]
    shape_all = (block_count, order_index.shape[0], cycle_count)
    unit_array = jnp.ones(shape_all, jnp.float32)
    zero_array = jnp.zeros(shape_all, jnp.float32)

    def product_half(half_turn, matrices):
        upper_left, upper_right, lower_left, lower_right, log_scale = matrices
        for inner_step in range(8):
            degree = block_base + (half_turn * 8 + inner_step).astype(jnp.float32)
            diag_top, off_top, off_low, diag_low = step_entries(degree, order_col, cosines)
            next_ul = diag_top * upper_left + off_top * lower_left
            next_ur = diag_top * upper_right + off_top * lower_right
            next_ll = off_low * upper_left + diag_low * lower_left
            next_lr = off_low * upper_right + diag_low * lower_right
            largest = jnp.maximum(jnp.maximum(jnp.abs(next_ul), jnp.abs(next_ur)), jnp.maximum(jnp.abs(next_ll), jnp.abs(next_lr)))
            upper_left = next_ul / largest
            upper_right = next_ur / largest
            lower_left = next_ll / largest
            lower_right = next_lr / largest
            log_scale = log_scale + jnp.log(largest)
        return (upper_left, upper_right, lower_left, lower_right, log_scale)
    products = lax.fori_loop(0, 2, product_half, (unit_array, zero_array, zero_array, unit_array, zero_array))

    def carry_block(vector_state, block_matrix):
        lead_value, lag_value, log_value = vector_state
        upper_left, upper_right, lower_left, lower_right, log_scale = block_matrix
        next_lead = upper_left * lead_value + upper_right * lag_value
        next_lag = lower_left * lead_value + lower_right * lag_value
        largest = jnp.maximum(jnp.abs(next_lead), jnp.abs(next_lag))
        return ((next_lead / largest, next_lag / largest, log_value + log_scale + jnp.log(largest)), vector_state)
    initial = (unit_array[0], zero_array[0], start_log)
    final_state, starts = lax.scan(carry_block, initial, products)

    def degree_half(vector_state, half_turn):
        lead_value, lag_value, log_value = vector_state
        values = []
        for inner_step in range(8):
            degree = block_base + (half_turn * 8 + inner_step).astype(jnp.float32)
            diag_top, off_top, off_low, diag_low = step_entries(degree, order_col, cosines)
            next_lead = diag_top * lead_value + off_top * lag_value
            next_lag = off_low * lead_value + diag_low * lag_value
            largest = jnp.maximum(jnp.abs(next_lead), jnp.abs(next_lag))
            lead_value = next_lead / largest
            lag_value = next_lag / largest
            log_value = log_value + jnp.log(largest)
            values.append(lead_value * jnp.exp(log_value))
        return ((lead_value, lag_value, log_value), jnp.stack(values))
    last_state, table_rows = lax.scan(degree_half, starts, jnp.arange(2, dtype=jnp.int32))
    legendre = jnp.transpose(table_rows, (3, 2, 0, 1, 4)).reshape(order_index.shape[0], degree_count, cycle_count)
    degrees = jnp.arange(degree_count, dtype=jnp.int32)
    return jnp.where(degrees[None, :, None] >= order_index[:, None, None], legendre, 0.0)

def layer_norm(values, gain_row):
    values = values.astype(jnp.float32)
    average = lax.optimization_barrier(jnp.mean(values, axis=-2, keepdims=True))
    centred = values - average
    variance = lax.optimization_barrier(jnp.mean(centred * centred, axis=-2, keepdims=True))
    return centred * lax.rsqrt(variance + EPSILON) * gain_row.astype(jnp.float32)[:, None]

def mixing_matrix(weight):
    width = weight.shape[1]
    real_weight = weight[:, :, :width]
    imag_weight = weight[:, :, width:]
    top_half = jnp.concatenate([real_weight, imag_weight], axis=2)
    bottom_half = jnp.concatenate([-imag_weight, real_weight], axis=2)
    return jnp.concatenate([top_half, bottom_half], axis=1)

def section_block(grid_values, spectral_row, weight, mixer_row, up_matrix, bias_row, down_matrix, legendre, forward, inverse, cycle_weight):
    normed = layer_norm(grid_values, spectral_row).astype(jnp.bfloat16)
    spectral = jnp.einsum('nrm,acn->marc', forward.astype(jnp.float32), normed.astype(jnp.float32))
    spectral = (spectral * cycle_weight[None, :, None, None]).astype(jnp.bfloat16).reshape(MMAX, NLAT, 2 * C)
    legendre_real = legendre.astype(jnp.float32)
    coeffs = jnp.einsum('mla,mak->mlk', legendre_real, spectral.astype(jnp.float32)).astype(jnp.bfloat16)
    block_weight = mixing_matrix(weight)
    mixed = jnp.einsum('mlk,lkj->mlj', coeffs.astype(jnp.float32), block_weight.astype(jnp.float32)).astype(jnp.bfloat16)
    grid_part = jnp.einsum('mla,mlk->mak', legendre_real, mixed.astype(jnp.float32)).astype(jnp.bfloat16)
    synthesis = jnp.einsum('marc,rmn->acn', grid_part.reshape(MMAX, NLAT, 2, C).astype(jnp.float32), inverse.astype(jnp.float32))
    residual = grid_values.astype(jnp.float32) + synthesis
    hidden_in = layer_norm(residual, mixer_row).astype(jnp.bfloat16)
    hidden = jnp.einsum('acn,ch->anh', hidden_in.astype(jnp.float32), up_matrix.astype(jnp.float32)) + bias_row.astype(jnp.float32)
    hidden = jax.nn.gelu(hidden, approximate=False).astype(jnp.bfloat16)
    branch = jnp.einsum('anh,ch->acn', hidden.astype(jnp.float32), down_matrix.astype(jnp.float32))
    return (residual + branch).astype(jnp.bfloat16)

def reference(field_in, spectral_gain, spectral_weight, mixer_gain, up_weight, up_bias, down_weight):
    all_orders = jnp.arange(MMAX, dtype=jnp.int32)
    legendre = legendre_rows(all_orders, NLAT, LMAX).astype(jnp.bfloat16)
    forward, inverse = fourier_tables(NLON, all_orders)
    cycle_weight = quad_weights(jnp.arange(NLAT, dtype=jnp.int32), NLAT) * (2.0 * math.pi / NLON)

    def one_section(section_args):
        grid_values, spectral_row, weight, mixer_row, up_matrix, bias_row, down_matrix = section_args
        return section_block(grid_values, spectral_row, weight, mixer_row, up_matrix, bias_row, down_matrix, legendre, forward, inverse, cycle_weight)
    outputs = lax.map(one_section, (field_in, spectral_gain, spectral_weight, mixer_gain, up_weight, up_bias, down_weight))
    return jnp.roll(outputs, 1, axis=0)
```

```python
import math

import jax
import jax.numpy as jnp
from jax import lax
from jax.sharding import PartitionSpec as P

C = 192
NLAT = 384
NLON = 768
LMAX = 384
MMAX = 384
CHUNKS = 4


EPSILON = 1e-05


def passed_along(value, axis, by):
    count = lax.axis_size(axis)
    return lax.ppermute(value, axis, [(i, (i + by) % count) for i in range(count)])


def quad_weights(cycle_index, cycle_count):
    terms_count = cycle_count // 2
    orders = jnp.arange(1, terms_count + 1, dtype=jnp.int32)
    phase_turns = orders[None, :] * (2 * cycle_index[:, None] + 1) % (2 * cycle_count)
    angles = math.pi * phase_turns.astype(jnp.float32) / cycle_count
    orders_real = orders.astype(jnp.float32)
    series = jnp.sum(jnp.cos(angles) / (4.0 * orders_real * orders_real - 1.0)[None, :], axis=1)
    return 2.0 / cycle_count * (1.0 - 2.0 * series)


def fourier_tables(point_count, orders):
    points = jnp.arange(point_count, dtype=jnp.int32)
    phase_turns = points[:, None] * orders[None, :] % point_count
    angles = 2.0 * math.pi / point_count * phase_turns.astype(jnp.float32)
    cosines = jnp.cos(angles)
    sine_values = jnp.sin(angles)
    forward = jnp.stack([cosines, -sine_values], axis=1).astype(jnp.bfloat16)
    doubling = jnp.where(orders == 0, 1.0, 2.0).astype(jnp.float32)[:, None]
    inverse = jnp.stack([cosines.T * doubling, -sine_values.T * doubling], axis=0).astype(
        jnp.bfloat16
    )
    return (forward, inverse)


def step_entries(degree, order_col, cosines):
    active = degree >= order_col + 1.0
    further = degree >= order_col + 2.0
    degree_sq = degree * degree
    order_sq = order_col * order_col
    lead_coeff = jnp.sqrt(
        jnp.where(
            active, (4.0 * degree_sq - 1.0) / jnp.where(active, degree_sq - order_sq, 1.0), 0.0
        )
    )
    before = degree - 1.0
    before_sq = before * before
    trail_coeff = jnp.sqrt(
        jnp.where(
            further, (before_sq - order_sq) / jnp.where(further, 4.0 * before_sq - 1.0, 1.0), 0.0
        )
    )
    diag_top = jnp.where(active, lead_coeff * cosines, 1.0)
    off_top = jnp.where(active, -lead_coeff * trail_coeff, 0.0)
    off_low = jnp.where(active, 1.0, 0.0)
    diag_low = jnp.where(active, 0.0, 1.0)
    return (diag_top, off_top, off_low, diag_low)


def legendre_rows(order_index, cycle_count, degree_count):
    colatitude = math.pi * (jnp.arange(cycle_count, dtype=jnp.float32) + 0.5) / cycle_count
    cosines = jnp.cos(colatitude)[None, None, :]
    sine_values = jnp.sin(colatitude)
    order_real = order_index.astype(jnp.float32)
    steps_all = jnp.arange(1, degree_count + 1, dtype=jnp.float32)
    factors = jnp.log((2.0 * steps_all - 1.0) / (2.0 * steps_all))
    below_mask = (steps_all[None, :] <= order_real[:, None]).astype(jnp.float32)
    partial_log = jnp.sum(below_mask * factors[None, :], axis=1)
    start_log = 0.5 * jnp.log((2.0 * order_real + 1.0) / (4.0 * math.pi)) + 0.5 * partial_log
    start_log = start_log[:, None] + order_real[:, None] * jnp.log(sine_values)[None, :]
    order_col = order_real[None, :, None]
    block_count = degree_count // 16
    block_base = (16 * jnp.arange(block_count, dtype=jnp.int32)).astype(jnp.float32)[:, None, None]
    shape_all = (block_count, order_index.shape[0], cycle_count)
    unit_array = jnp.ones(shape_all, jnp.float32)
    zero_array = jnp.zeros(shape_all, jnp.float32)

    def product_half(half_turn, matrices):
        upper_left, upper_right, lower_left, lower_right, log_scale = matrices
        for inner_step in range(8):
            degree = block_base + (half_turn * 8 + inner_step).astype(jnp.float32)
            diag_top, off_top, off_low, diag_low = step_entries(degree, order_col, cosines)
            next_ul = diag_top * upper_left + off_top * lower_left
            next_ur = diag_top * upper_right + off_top * lower_right
            next_ll = off_low * upper_left + diag_low * lower_left
            next_lr = off_low * upper_right + diag_low * lower_right
            largest = jnp.maximum(
                jnp.maximum(jnp.abs(next_ul), jnp.abs(next_ur)),
                jnp.maximum(jnp.abs(next_ll), jnp.abs(next_lr)),
            )
            upper_left = next_ul / largest
            upper_right = next_ur / largest
            lower_left = next_ll / largest
            lower_right = next_lr / largest
            log_scale = log_scale + jnp.log(largest)
        return (upper_left, upper_right, lower_left, lower_right, log_scale)

    products = lax.fori_loop(
        0, 2, product_half, (unit_array, zero_array, zero_array, unit_array, zero_array)
    )

    def carry_block(vector_state, block_matrix):
        lead_value, lag_value, log_value = vector_state
        upper_left, upper_right, lower_left, lower_right, log_scale = block_matrix
        next_lead = upper_left * lead_value + upper_right * lag_value
        next_lag = lower_left * lead_value + lower_right * lag_value
        largest = jnp.maximum(jnp.abs(next_lead), jnp.abs(next_lag))
        return (
            (next_lead / largest, next_lag / largest, log_value + log_scale + jnp.log(largest)),
            vector_state,
        )

    initial = (unit_array[0], zero_array[0], start_log)
    final_state, starts = lax.scan(carry_block, initial, products)

    def degree_half(vector_state, half_turn):
        lead_value, lag_value, log_value = vector_state
        values = []
        for inner_step in range(8):
            degree = block_base + (half_turn * 8 + inner_step).astype(jnp.float32)
            diag_top, off_top, off_low, diag_low = step_entries(degree, order_col, cosines)
            next_lead = diag_top * lead_value + off_top * lag_value
            next_lag = off_low * lead_value + diag_low * lag_value
            largest = jnp.maximum(jnp.abs(next_lead), jnp.abs(next_lag))
            lead_value = next_lead / largest
            lag_value = next_lag / largest
            log_value = log_value + jnp.log(largest)
            values.append(lead_value * jnp.exp(log_value))
        return ((lead_value, lag_value, log_value), jnp.stack(values))

    last_state, table_rows = lax.scan(degree_half, starts, jnp.arange(2, dtype=jnp.int32))
    legendre = jnp.transpose(table_rows, (3, 2, 0, 1, 4)).reshape(
        order_index.shape[0], degree_count, cycle_count
    )
    degrees = jnp.arange(degree_count, dtype=jnp.int32)
    return jnp.where(degrees[None, :, None] >= order_index[:, None, None], legendre, 0.0)


def layer_norm(values, gain_row):
    values = values.astype(jnp.float32)
    average = jnp.mean(values, axis=-2, keepdims=True)
    centred = values - average
    variance = jnp.mean(centred * centred, axis=-2, keepdims=True)
    return centred * lax.rsqrt(variance + EPSILON) * gain_row.astype(jnp.float32)[:, None]


def mixing_matrix(weight):
    width = weight.shape[1]
    real_weight = weight[:, :, :width]
    imag_weight = weight[:, :, width:]
    top_half = jnp.concatenate([real_weight, imag_weight], axis=2)
    bottom_half = jnp.concatenate([-imag_weight, real_weight], axis=2)
    return jnp.concatenate([top_half, bottom_half], axis=1)


def order_list(sp_count, modes_dev):
    slots = jnp.arange(MMAX, dtype=jnp.int32)
    owner = slots // modes_dev
    within = slots % modes_dev
    mirrored = jnp.where(within % 2 == 0, owner, sp_count - 1 - owner)
    return within * sp_count + mirrored


def triangle_plan(sp_count, half):
    plan = []
    for rank in range(sp_count):
        low_block = min(rank, sp_count - 1 - rank)
        high_block = sp_count - 1 - low_block
        low_half = 0 if rank == low_block else 1
        low_start = (2 * low_block + low_half) * half
        high_start = (2 * high_block + 1 - low_half) * half
        low_count = (low_start + half - 1) // sp_count + 1
        high_count = (high_start + half - 1) // sp_count + 1
        plan.append((low_start, low_count, high_start, high_count))
    slots = max(entry[1] + entry[3] for entry in plan)
    return (plan, slots)


def shards(field_in, spectral_gain, spectral_weight, mixer_gain, up_weight, up_bias, down_weight):
    grid_values = field_in[0]
    cycle_rows = grid_values.shape[0]
    sp_count = lax.axis_size("sp")
    device_rank = lax.axis_index("sp")
    modes_dev = MMAX // sp_count
    all_orders = order_list(sp_count, modes_dev)
    order_index = lax.dynamic_slice_in_dim(all_orders, device_rank * modes_dev, modes_dev, 0)
    cycle_index = device_rank * cycle_rows + jnp.arange(cycle_rows, dtype=jnp.int32)
    legendre = legendre_rows(order_index, NLAT, LMAX).astype(jnp.bfloat16)
    forward, inverse = fourier_tables(NLON, all_orders)
    weighting = quad_weights(cycle_index, NLAT) * (2.0 * math.pi / NLON)
    normed = layer_norm(grid_values, spectral_gain[0]).astype(jnp.bfloat16)
    spectral = jnp.einsum("nrm,acn->marc", forward, normed, preferred_element_type=jnp.float32)
    spectral = (
        (spectral * weighting[None, :, None, None])
        .astype(jnp.bfloat16)
        .reshape(MMAX, cycle_rows, 2 * C)
    )
    coeffs = jnp.einsum(
        "mla,mak->mlk",
        legendre,
        lax.all_to_all(spectral, "sp", split_axis=0, concat_axis=1, tiled=True),
        preferred_element_type=jnp.float32,
    ).astype(jnp.bfloat16)
    half = LMAX // sp_count // 2
    plan, slots = triangle_plan(sp_count, half)
    own_weight = spectral_weight[0]
    partner = [(i, sp_count - 1 - i) for i in range(sp_count)]
    other_weight = lax.ppermute(own_weight[half:], "sp", partner)
    is_low = device_rank < sp_count // 2
    low_weight = mixing_matrix(jnp.where(is_low, own_weight[:half], other_weight))
    high_weight = mixing_matrix(jnp.where(is_low, other_weight, own_weight[:half]))
    width = coeffs.shape[2]
    pieces = []
    for low_start, low_count, high_start, high_count in plan:
        pieces.append(coeffs[:low_count, low_start : low_start + half])
        gap = slots - low_count - high_count
        if gap:
            pieces.append(jnp.zeros((gap, half, width), coeffs.dtype))
        pieces.append(coeffs[:high_count, high_start : high_start + half])
    packed = jnp.concatenate(pieces, axis=0)
    by_degree = lax.all_to_all(packed, "sp", split_axis=0, concat_axis=0, tiled=True)
    by_degree = by_degree.reshape(sp_count, slots, half, width)
    most_low = max(entry[1] for entry in plan)
    most_high = max(entry[3] for entry in plan)
    low_mixed = jnp.einsum(
        "dslk,lkj->dslj",
        by_degree[:, :most_low],
        low_weight,
        preferred_element_type=jnp.float32,
    ).astype(jnp.bfloat16)
    high_mixed = jnp.einsum(
        "dslk,lkj->dslj",
        by_degree[:, slots - most_high :],
        high_weight,
        preferred_element_type=jnp.float32,
    ).astype(jnp.bfloat16)
    low_rows = jnp.array([entry[1] for entry in plan], jnp.int32)[device_rank]
    row = jnp.arange(slots, dtype=jnp.int32)[None, :, None, None]
    mixed = jnp.where(
        row < low_rows,
        jnp.pad(low_mixed, ((0, 0), (0, slots - most_low), (0, 0), (0, 0))),
        jnp.pad(high_mixed, ((0, 0), (slots - most_high, 0), (0, 0), (0, 0))),
    )
    returned = lax.all_to_all(
        mixed.reshape(sp_count * slots, half, width),
        "sp",
        split_axis=0,
        concat_axis=0,
        tiled=True,
    ).reshape(sp_count, slots, half, width)
    parts = {}
    for rank, (low_start, low_count, high_start, high_count) in enumerate(plan):
        parts[low_start] = (returned[rank, :low_count], low_count)
        parts[high_start] = (returned[rank, slots - high_count :], high_count)
    mixed_coeffs = jnp.concatenate(
        [
            jnp.pad(parts[start][0], ((0, modes_dev - parts[start][1]), (0, 0), (0, 0)))
            for start in sorted(parts)
        ],
        axis=1,
    )
    grid_part = jnp.einsum(
        "mla,mlk->mak", legendre, mixed_coeffs, preferred_element_type=jnp.float32
    ).astype(jnp.bfloat16)
    grid_part = grid_part.reshape(modes_dev, sp_count, cycle_rows, width)
    chunk = cycle_rows // CHUNKS
    outputs = []
    for start in range(0, cycle_rows, chunk):
        on_grid = lax.all_to_all(
            grid_part[:, :, start : start + chunk].reshape(modes_dev, sp_count * chunk, width),
            "sp",
            split_axis=1,
            concat_axis=0,
            tiled=True,
        )
        synthesis = jnp.einsum(
            "marc,rmn->acn",
            on_grid.reshape(MMAX, chunk, 2, C),
            inverse,
            preferred_element_type=jnp.float32,
        )
        residual = grid_values[start : start + chunk].astype(jnp.float32) + synthesis
        hidden_in = layer_norm(residual, mixer_gain[0]).astype(jnp.bfloat16)
        hidden = jnp.einsum(
            "acn,ch->anh", hidden_in, up_weight[0], preferred_element_type=jnp.float32
        ) + up_bias[0].astype(jnp.float32)
        hidden = jax.nn.gelu(hidden, approximate=False).astype(jnp.bfloat16)
        branch = jnp.einsum(
            "anh,ch->acn", hidden, down_weight[0], preferred_element_type=jnp.float32
        )
        result = (residual + branch).astype(jnp.bfloat16)
        outputs.append(passed_along(result, "section", 1))
    return jnp.concatenate(outputs, axis=0)[None]


def solution(mesh):
    in_specs = (
        P("section", "sp", None, None),
        P("section", None),
        P("section", "sp", None, None),
        P("section", None),
        P("section", None, None),
        P("section", None),
        P("section", None, None),
    )
    out_specs = P("section", "sp", None, None)
    return jax.shard_map(shards, mesh=mesh, in_specs=in_specs, out_specs=out_specs, check_vma=False)
```
